32 devices in a mesh: section: 2 (over y), dp: 4 (over x, core), tensor: 4 (over z).
Axes of the slice: x: 2, y: 2, z: 4, core: 2. Of those that a mesh axis runs over, the one named last changes fastest.
Arguments:
- acts_in: bfloat16 [4, 1024, 4, 1024], P(None, 'tensor', 'dp'), may hold values from -6 to 6
- cotangent: bfloat16 [4, 1024, 4, 1024], P(None, 'tensor', 'dp'), may hold values from -6 to 6
- norm_gains: float32 [2, 2, 1024], P('section', None, ('dp', 'tensor')), may hold values from 0.5 to 1.5
- vec_bias: float32 [2, 4, 1024], P('section', None, ('dp', 'tensor')), may hold values from -1.8 to 1.8
- w_qkv: bfloat16 [2, 1024, 3072], P('section', 'dp', 'tensor'), may hold values from -0.25 to 0.25
- b_qkv: bfloat16 [2, 16, 192], P('section', 'tensor', 'dp'), may hold values from -1.796875 to 1.796875
- w_out: bfloat16 [2, 1024, 1024], P('section', 'tensor', 'dp'), may hold values from -0.75 to 0.75
- w_up: bfloat16 [2, 1024, 4096], P('section', 'dp', 'tensor'), may hold values from -0.1875 to 0.1875
- b_up: bfloat16 [2, 32, 128], P('section', 'tensor', 'dp'), may hold values from -1.796875 to 1.796875
- w_down: bfloat16 [2, 4096, 1024], P('section', 'tensor', 'dp'), may hold values from -0.09375 to 0.09375
Outputs:
- acts_out: bfloat16 [2, 4, 1024, 4, 1024], P('section', None, 'tensor', 'dp')
- grad_in: bfloat16 [2, 4, 1024, 4, 1024], P('section', None, 'tensor', 'dp')
- grad_norm_gains: float32 [2, 2, 1024], P('section', None, ('dp', 'tensor'))
- grad_vec_bias: float32 [2, 4, 1024], P('section', None, ('dp', 'tensor'))
- grad_w_qkv: float32 [2, 1024, 3072], P('section', 'dp', 'tensor')
- grad_b_qkv: float32 [2, 16, 192], P('section', 'tensor', 'dp')
- grad_w_out: float32 [2, 1024, 1024], P('section', 'tensor', 'dp')
- grad_w_up: float32 [2, 1024, 4096], P('section', 'dp', 'tensor')
- grad_b_up: float32 [2, 32, 128], P('section', 'tensor', 'dp')
- grad_w_down: float32 [2, 4096, 1024], P('section', 'tensor', 'dp')
The draws below stay inside these ranges and needn't reach their ends.
All inputs are finite; a program needn't handle non-finite values.
Results may differ from the reference program's by a relative error of at most 0.025.
Values may be sent and summed in bfloat16 or wider, within the bound.
No kernel may reach another device: no remote copies, remote signals or barrier semaphores. Data moves between devices by JAX's collectives and lax.ppermute only.
A program may use at most 384 MiB of HBM per device.

```python
import math
import jax
import jax.numpy as jnp
from jax import lax

D = 1024
HEADS = 16
DH = 64
ROT = 16
FF = 4096
BIAS_COLS = 128
SEQ_LEN = 1024
QBLOCK = 512
MICRO = 4
SECTIONS = 2
SEQS = 4


def steps_of(own_key, extent, cuts, low, largest):
    level = 1.0
    for axis_at, parts in cuts:
        draws = jax.random.uniform(jax.random.fold_in(jax.random.fold_in(own_key, 6), axis_at), (parts,), jnp.float32, low / len(cuts), largest / len(cuts))
        level = level * jnp.repeat(jnp.exp(draws), extent[axis_at] // parts).reshape((-1,) + (1,) * (len(extent) - 1 - axis_at))
    return level


def noise(rng, extent, scale, bound, cuts=(), kind=jnp.bfloat16):
    factor_of = steps_of(rng, extent, cuts, -0.22, 0.18) if cuts else 1.0
    drawn = jax.random.normal(rng, extent, jnp.float32) * scale * factor_of
    return jnp.minimum(jnp.maximum(drawn, -bound), bound).astype(kind)


def setup_inputs(seed: int = 0) -> dict:
    key_list = jax.random.split(jax.random.key(seed), 11)
    acts_in = noise(key_list[0], (MICRO, SEQ_LEN, SEQS, D), 1.0, 6.0, ((1, 4), (2, 4)))
    cotangent = noise(key_list[1], (MICRO, SEQ_LEN, SEQS, D), 1.0, 6.0, ((1, 4), (2, 4)))
    norm_gains = jnp.clip(1.0 + 0.1 * jax.random.normal(key_list[2], (SECTIONS, 2, D), jnp.float32), 0.5, 1.5)
    vec_bias = noise(key_list[3], (SECTIONS, 4, D), 0.3, 1.8, ((0, 2), (2, 16)), jnp.float32)
    w_qkv = noise(key_list[4], (SECTIONS, D, 3 * D), (D // 2) ** -0.5, 0.25, ((0, 2), (1, 4), (2, 4)))
    b_qkv = noise(key_list[5], (SECTIONS, HEADS, 3 * DH), 0.3, 1.796875, ((0, 2), (1, 4), (2, 4)))
    w_out = noise(key_list[6], (SECTIONS, D, D), (D // 16) ** -0.5, 0.75, ((0, 2), (1, 4), (2, 4)))
    w_up = noise(key_list[7], (SECTIONS, D, FF), D ** -0.5, 0.1875, ((0, 2), (1, 4), (2, 4)))
    b_up = noise(key_list[8], (SECTIONS, FF // BIAS_COLS, BIAS_COLS), 0.3, 1.796875, ((0, 2), (1, 4), (2, 4)))
    w_down = noise(key_list[9], (SECTIONS, FF, D), FF ** -0.5, 0.09375, ((0, 2), (1, 4), (2, 4)))
    return dict(acts_in=acts_in, cotangent=cotangent, norm_gains=norm_gains, vec_bias=vec_bias, w_qkv=w_qkv, b_qkv=b_qkv, w_out=w_out, w_up=w_up, b_up=b_up, w_down=w_down)


HIGHEST = lax.Precision.HIGHEST
NORM_EPS = 1e-05
ROPE_BASE = 10000.0
MASK_FILL = -1e+30

@jax.custom_vjp
def low(v):
    return lax.optimization_barrier(v.astype(jnp.bfloat16)).astype(jnp.float32)

@jax.custom_vjp
def low_back(v):
    return v

def low_keep(v):
    return (low(v), None)

def low_pass(kept, grad):
    return (grad,)

def back_keep(v):
    return (v, None)

def back_low(kept, grad):
    return (low(grad),)
low.defvjp(low_keep, low_pass)
low_back.defvjp(back_keep, back_low)

def layer_norm(values, norm_gain, norm_shift):
    average = lax.optimization_barrier(jnp.mean(values, axis=-1, keepdims=True))
    centred = values - average
    variance = lax.optimization_barrier(jnp.mean(centred * centred, axis=-1, keepdims=True))
    return centred * lax.rsqrt(variance + NORM_EPS) * norm_gain + norm_shift

def rotary_tables(length):
    half_rot = ROT // 2
    frequency = jnp.exp(jnp.arange(half_rot, dtype=jnp.float32) * (-2.0 * math.log(ROPE_BASE) / ROT))
    angles = jnp.arange(length, dtype=jnp.float32)[:, None] * frequency[None, :]
    return (jnp.cos(angles), jnp.sin(angles))

def rotate(values, cosine, sine_tab):
    half_rot = ROT // 2
    low_half = values[..., :half_rot]
    high_half = values[..., half_rot:ROT]
    return jnp.concatenate([low_half * cosine - high_half * sine_tab, high_half * cosine + low_half * sine_tab, values[..., ROT:]], axis=-1)

def matmul(left, right):
    return jnp.einsum('...d,de->...e', left, right, precision=HIGHEST)

def attention(queries, key_rows, val_rows):
    batch, length, head_count, head_dim = queries.shape
    block_rows = min(QBLOCK, length)
    block_count = length // block_rows
    score_scale = head_dim ** (-0.5)
    query_blocks = queries.reshape(batch, block_count, block_rows, head_count, head_dim).transpose(1, 0, 2, 3, 4)
    block_starts = jnp.arange(block_count, dtype=jnp.int32) * block_rows
    key_pos = jnp.arange(length, dtype=jnp.int32)

    @jax.checkpoint
    def one_block(pieces):
        query_block, first_row = pieces
        scores = low_back(score_scale * jnp.einsum('bqhd,bkhd->bhqk', query_block, key_rows, precision=HIGHEST))
        row_pos = first_row + jnp.arange(block_rows, dtype=jnp.int32)
        allowed = key_pos[None, :] <= row_pos[:, None]
        scores = jnp.where(allowed, scores, MASK_FILL)
        probability = low(jax.nn.softmax(scores, axis=-1))
        return jnp.einsum('bhqk,bkhd->bqhd', probability, val_rows, precision=HIGHEST)
    blocks_out = lax.map(one_block, (query_blocks, block_starts))
    return blocks_out.transpose(1, 0, 2, 3, 4).reshape(batch, length, head_count * head_dim)

def layer_forward(values, params):
    norm_gain, vector_bias, mat_qkv, bias_qkv, mat_out, mat_up, bias_up, mat_down = params
    batch, length, model_width = values.shape
    head_count = bias_qkv.shape[0]
    head_dim = bias_qkv.shape[1] // 3
    normed_attn = low(layer_norm(values, norm_gain[0], vector_bias[0]))
    normed_mlp = low(layer_norm(values, norm_gain[1], vector_bias[1]))
    projected = low_back(matmul(normed_attn, mat_qkv) + bias_qkv.reshape(-1))
    projected = projected.reshape(batch, length, head_count, 3, head_dim)
    cosine, sine_tab = rotary_tables(length)
    cosine = cosine[None, :, None, :]
    sine_tab = sine_tab[None, :, None, :]
    queries = low(rotate(projected[:, :, :, 0], cosine, sine_tab))
    key_rows = low(rotate(projected[:, :, :, 1], cosine, sine_tab))
    val_rows = low(projected[:, :, :, 2])
    context = low_back(low(attention(queries, key_rows, val_rows)))
    up_proj = low_back(matmul(normed_mlp, mat_up) + bias_up.reshape(-1))
    activated = low(jax.nn.gelu(up_proj, approximate=False))
    return values + matmul(context, mat_out) + vector_bias[2] + matmul(activated, mat_down) + vector_bias[3]

def reference(acts_in, cotangent, norm_gains, vec_bias, w_qkv, b_qkv, w_out, w_up, b_up, w_down):
    params = tuple((item.astype(jnp.float32) for item in (norm_gains, vec_bias, w_qkv, b_qkv, w_out, w_up, b_up, w_down)))
    first_params = tuple((item[0] for item in params))
    second_params = tuple((item[1] for item in params))
    seq_total = MICRO * SEQS
    inputs = acts_in.transpose(0, 2, 1, 3).reshape(seq_total, SEQ_LEN, D)
    cot_rows = cotangent.transpose(0, 2, 1, 3).reshape(seq_total, SEQ_LEN, D)

    def two_layers(first_in, offset, params_one, params_two):
        first_out = layer_forward(first_in, params_one)
        handoff = low_back(low(first_out))
        return (handoff, layer_forward(handoff + offset, params_two))

    def one_sequence(running, sequence):
        seq_in, seq_cot = sequence
        seq_in = seq_in.astype(jnp.float32)[None]
        seq_cot = seq_cot.astype(jnp.float32)[None]
        offset = jnp.zeros_like(seq_in)
        (handoff, second_out), pullback = jax.vjp(two_layers, seq_in, offset, first_params, second_params)
        grad_first, grad_offset, grads_one, grads_two = pullback((jnp.zeros_like(handoff), seq_cot))
        running = jax.tree.map(lambda c, a, b: c + jnp.stack([a, b]), running, grads_one, grads_two)
        return (running, (handoff[0].astype(jnp.bfloat16), second_out[0].astype(jnp.bfloat16), grad_first[0].astype(jnp.bfloat16), grad_offset[0].astype(jnp.bfloat16)))
    zeros_init = tuple((jnp.zeros_like(item) for item in params))
    gradients, (handoffs, seconds, grads_first, grads_offset) = lax.scan(one_sequence, zeros_init, (inputs, cot_rows))

    def arrange(stacked):
        return stacked.reshape(MICRO, SEQS, SEQ_LEN, D).transpose(0, 2, 1, 3)
    acts_out = jnp.stack([arrange(handoffs), arrange(seconds)])
    grad_in = jnp.stack([arrange(grads_first), arrange(grads_offset)])
    return (acts_out, grad_in, gradients[0], gradients[1], gradients[2], gradients[3], gradients[4], gradients[5], gradients[6], gradients[7])
```

```python
import math

import jax
import jax.numpy as jnp
from jax import lax
from jax.experimental import pallas as pl
from jax.experimental.pallas import tpu as pltpu
from jax.sharding import Mesh
from jax.sharding import PartitionSpec as P

ROT = 16
NORM_EPS = 1e-05
ROPE_BASE = 10000.0
MASK_FILL = -1e30
BLOCK = 256
PAIR = 2
F32 = jnp.float32
BF16 = jnp.bfloat16


def rotation_tables(length, head_dim):
    half = ROT // 2
    frequency = jnp.exp(jnp.arange(half, dtype=F32) * (-2.0 * math.log(ROPE_BASE) / ROT))
    angles = jnp.arange(length, dtype=F32)[:, None] * frequency[None, :]
    cosine, sine = jnp.cos(angles), jnp.sin(angles)
    zero = jnp.zeros_like(sine)
    rest = jnp.zeros((length, head_dim - ROT), F32)
    keep_part = jnp.concatenate([cosine, cosine, rest + 1.0], axis=1)
    ahead_part = jnp.concatenate([-sine, zero, rest], axis=1)
    behind_part = jnp.concatenate([zero, sine, rest], axis=1)
    plain = jnp.zeros((length, head_dim), F32)

    def widen(part, value_part):
        return jnp.concatenate([part, part, value_part] * PAIR, axis=1)

    return (
        widen(keep_part, plain + 1.0),
        widen(ahead_part, plain),
        widen(behind_part, plain),
    )


def turn(values, keep, ahead, behind, sign):
    width = values.shape[1]
    half = ROT // 2
    moved = pltpu.roll(values, width - half, 1) * ahead + pltpu.roll(values, half, 1) * behind
    return values * keep + moved * sign


def rows_dot(left, right):
    return lax.dot_general(left, right, (((1,), (1,)), ((), ())), preferred_element_type=F32)


def attend_kernel(qkv_ref, keep_ref, ahead_ref, behind_ref, out_ref):
    length = qkv_ref.shape[1]
    head_dim = out_ref.shape[1] // PAIR
    block = min(BLOCK, length)
    turned = turn(qkv_ref[0].astype(F32), keep_ref[...], ahead_ref[...], behind_ref[...], 1.0)
    scale = head_dim ** (-0.5)
    parts = []
    for head in range(PAIR):
        base = head * 3 * head_dim
        queries = (turned[:, base : base + head_dim].astype(BF16).astype(F32) * scale).astype(BF16)
        key_rows = turned[:, base + head_dim : base + 2 * head_dim].astype(BF16)
        val_rows = turned[:, base + 2 * head_dim : base + 3 * head_dim].astype(BF16)
        parts.append((queries, key_rows, val_rows))
    row = lax.broadcasted_iota(jnp.int32, (block, block), 0)
    col = lax.broadcasted_iota(jnp.int32, (block, block), 1)
    allowed = col <= row
    for start in range(0, length, block):
        stop = start + block
        outs = []
        for queries, key_rows, val_rows in parts:
            scores = rows_dot(queries[start:stop], key_rows[:stop])
            edge = jnp.where(allowed, scores[:, start:], MASK_FILL)
            if start:
                scores = jnp.concatenate([scores[:, :start], edge], axis=1)
            else:
                scores = edge
            highest = jnp.max(scores, axis=1, keepdims=True)
            exponent = jnp.exp(scores - highest)
            inverse = 1.0 / jnp.sum(exponent, axis=1, keepdims=True)
            probability = (exponent * inverse).astype(BF16)
            outs.append(jnp.dot(probability, val_rows[:stop], preferred_element_type=F32))
        out_ref[start:stop, :] = jnp.concatenate(outs, axis=1).astype(BF16)


def attend_back_kernel(qkv_ref, dctx_ref, keep_ref, ahead_ref, behind_ref, out_ref, total):
    length = qkv_ref.shape[1]
    head_dim = dctx_ref.shape[1] // PAIR
    block = min(BLOCK, length)
    turned = turn(qkv_ref[0].astype(F32), keep_ref[...], ahead_ref[...], behind_ref[...], 1.0)
    scale = head_dim ** (-0.5)
    key_pos = lax.broadcasted_iota(jnp.int32, (block, block), 0)
    row_pos = lax.broadcasted_iota(jnp.int32, (block, block), 1)
    allowed = key_pos <= row_pos
    parts = []
    for head in range(PAIR):
        base = head * 3 * head_dim
        queries = (turned[:, base : base + head_dim].astype(BF16).astype(F32) * scale).astype(BF16)
        key_rows = turned[:, base + head_dim : base + 2 * head_dim].astype(BF16)
        val_rows = turned[:, base + 2 * head_dim : base + 3 * head_dim].astype(BF16)
        d_rows = dctx_ref[:, head * head_dim : (head + 1) * head_dim]
        parts.append((base, queries, key_rows, val_rows, d_rows))
    for start in reversed(range(0, length, block)):
        stop = start + block
        for base, queries, key_rows, val_rows, d_rows in parts:
            query_block = queries[start:stop]
            d_block = d_rows[start:stop]
            scores = rows_dot(key_rows[:stop], query_block)
            edge = jnp.where(allowed, scores[start:], MASK_FILL)
            if start:
                scores = jnp.concatenate([scores[:start], edge], axis=0)
            else:
                scores = edge
            highest = jnp.max(scores, axis=0, keepdims=True)
            exponent = jnp.exp(scores - highest)
            inverse = 1.0 / jnp.sum(exponent, axis=0, keepdims=True)
            probability = exponent * inverse
            d_prob = rows_dot(val_rows[:stop], d_block)
            delta = jnp.sum(probability * d_prob, axis=0, keepdims=True)
            d_scores = (probability * (d_prob - delta)).astype(BF16)
            d_keys = jnp.dot(d_scores, query_block, preferred_element_type=F32)
            d_vals = jnp.dot(probability.astype(BF16), d_block, preferred_element_type=F32)
            d_queries = lax.dot_general(
                key_rows[:stop], d_scores, (((0,), (0,)), ((), ())), preferred_element_type=F32
            )
            total[start:stop, base : base + head_dim] = d_queries.T * scale
            key_at = slice(base + head_dim, base + 2 * head_dim)
            val_at = slice(base + 2 * head_dim, base + 3 * head_dim)
            if stop == length:
                total[:stop, key_at] = d_keys
                total[:stop, val_at] = d_vals
            else:
                total[:stop, key_at] = total[:stop, key_at] + d_keys
                total[:stop, val_at] = total[:stop, val_at] + d_vals
    out_ref[0] = turn(total[...], keep_ref[...], ahead_ref[...], behind_ref[...], -1.0).astype(BF16)


def attention(qkv, tables, length, head_dim):
    groups, rows, width = qkv.shape
    wide = PAIR * 3 * head_dim
    pairs = width // wide
    table = pl.BlockSpec((length, wide), lambda t, n, p: (0, 0))
    work = groups * rows * pairs * PAIR * length * head_dim
    return pl.pallas_call(
        attend_kernel,
        out_shape=jax.ShapeDtypeStruct((rows, groups * pairs * PAIR * head_dim), BF16),
        grid=(groups, rows // length, pairs),
        in_specs=[pl.BlockSpec((1, length, wide), lambda t, n, p: (t, n, p))] + [table] * 3,
        out_specs=pl.BlockSpec((length, PAIR * head_dim), lambda t, n, p: (n, t * pairs + p)),
        cost_estimate=pl.CostEstimate(
            flops=4 * work, bytes_accessed=qkv.size * 3, transcendentals=work // head_dim
        ),
        name="attend",
    )(qkv, *tables)


def attention_back(qkv, d_context, tables, length, head_dim):
    groups, rows, width = qkv.shape
    wide = PAIR * 3 * head_dim
    pairs = width // wide
    table = pl.BlockSpec((length, wide), lambda t, n, p: (0, 0))
    work = groups * rows * pairs * PAIR * length * head_dim
    return pl.pallas_call(
        attend_back_kernel,
        out_shape=jax.ShapeDtypeStruct(qkv.shape, BF16),
        grid=(groups, rows // length, pairs),
        in_specs=[
            pl.BlockSpec((1, length, wide), lambda t, n, p: (t, n, p)),
            pl.BlockSpec((length, PAIR * head_dim), lambda t, n, p: (n, t * pairs + p)),
        ]
        + [table] * 3,
        out_specs=pl.BlockSpec((1, length, wide), lambda t, n, p: (t, n, p)),
        scratch_shapes=[pltpu.VMEM((length, wide), F32)],
        cost_estimate=pl.CostEstimate(
            flops=10 * work, bytes_accessed=qkv.size * 5, transcendentals=work // head_dim
        ),
        name="attend_back",
    )(qkv, d_context, *tables)


def product(equation, left, right):
    return jnp.einsum(equation, left, right, preferred_element_type=F32)


def statistics(values):
    average = jnp.mean(values, axis=-1, keepdims=True)
    centred = values - average
    variance = jnp.mean(centred * centred, axis=-1, keepdims=True)
    inverse = lax.rsqrt(variance + NORM_EPS)
    return centred * inverse, inverse


def forward(inputs, params, tables, length, head_dim):
    gains, shifts, mat_qkv, bias_qkv, mat_out, mat_up, bias_up, mat_down = params
    values = inputs.astype(F32)
    scaled, _ = statistics(values)
    normed_attn = (scaled * gains[0] + shifts[0]).astype(BF16)
    normed_mlp = (scaled * gains[1] + shifts[1]).astype(BF16)
    qkv = (product("sk,tke->tse", normed_attn, mat_qkv) + bias_qkv[:, None, :]).astype(BF16)
    context = attention(qkv, tables, length, head_dim)
    raised = product("sk,tke->ste", normed_mlp, mat_up) + bias_up
    below = 0.5 * lax.erf(raised * math.sqrt(0.5)) + 0.5
    active = (raised * below).astype(BF16)
    slope = (below + raised * jnp.exp(-0.5 * raised * raised) * (1.0 / math.sqrt(2.0 * math.pi))).astype(BF16)
    rows = inputs.shape[0]
    active = active.reshape(rows, -1)
    slope = slope.reshape(rows, -1)
    summed = product("sk,bkn->sbn", context, mat_out) + product("sk,bkn->sbn", active, mat_down)
    result = values + summed.reshape(rows, -1) + (shifts[2] + shifts[3])
    return result.astype(BF16), (normed_attn, normed_mlp, qkv, context, active, slope)


def backward(inputs, upstream, params, stash, tables, length, head_dim):
    gains, shifts, mat_qkv, bias_qkv, mat_out, mat_up, bias_up, mat_down = params
    normed_attn, normed_mlp, qkv, context, active, slope = stash
    rows = inputs.shape[0]
    pieces = mat_out.shape[0]
    groups = mat_qkv.shape[0]
    split = upstream.reshape(rows, pieces, -1)
    d_active = product("sbn,bkn->sk", split, mat_down)
    d_up = (d_active * slope.astype(F32)).astype(BF16)
    d_context = product("sbn,bkn->sk", split, mat_out).astype(BF16)
    d_up_split = d_up.reshape(rows, groups, -1)
    grad_down = product("sk,sbn->bkn", active, split)
    grad_up = product("sk,ste->tke", normed_mlp, d_up_split)
    d_qkv = attention_back(qkv, d_context, tables, length, head_dim)
    grad_out = product("sk,sbn->bkn", context, split)
    grad_qkv = product("sk,tse->tke", normed_attn, d_qkv)
    d_attn = product("tse,tke->sk", d_qkv, mat_qkv)
    d_mlp = product("ste,tke->sk", d_up_split, mat_up)
    scaled, inverse = statistics(inputs.astype(F32))
    d_scaled = d_attn * gains[0] + d_mlp * gains[1]
    term = inverse * (
        d_scaled
        - jnp.mean(d_scaled, axis=-1, keepdims=True)
        - scaled * jnp.mean(d_scaled * scaled, axis=-1, keepdims=True)
    )
    upstream_float = upstream.astype(F32)
    d_inputs = (upstream_float + term).astype(BF16)
    out_shift = jnp.sum(upstream_float, axis=0)
    small = (
        jnp.stack([jnp.sum(d_attn * scaled, axis=0), jnp.sum(d_mlp * scaled, axis=0)]),
        jnp.stack([jnp.sum(d_attn, axis=0), jnp.sum(d_mlp, axis=0), out_shift, out_shift]),
        jnp.sum(d_qkv.astype(F32), axis=1),
        jnp.sum(d_up_split.astype(F32), axis=0),
    )
    return d_inputs, (grad_qkv, grad_out, grad_up, grad_down), small


def swap_pairs(axis):
    return [(0, 1), (1, 0)]


def gather_stack(value, axis):
    if lax.axis_size(axis) == 2:
        other = lax.ppermute(value, axis, swap_pairs(axis))
        first = lax.axis_index(axis) == 0
        return jnp.stack([jnp.where(first, value, other), jnp.where(first, other, value)])
    return lax.all_gather(value, axis, axis=0, tiled=False)


def halve(value, axis):
    mine = lax.axis_index(axis)
    kept = lax.dynamic_index_in_dim(value, mine, 0, keepdims=False)
    sent = lax.dynamic_index_in_dim(value, 1 - mine, 0, keepdims=False).astype(BF16)
    came = lax.ppermute(sent, axis, swap_pairs(axis))
    return kept.astype(F32) + came.astype(F32)


def scatter_sum(value, axis):
    if lax.axis_size(axis) == 2:
        return halve(value, axis)
    return lax.psum_scatter(value.astype(BF16), axis, scatter_dimension=0, tiled=False).astype(F32)


def local(acts_in, cotangent, norm_gains, vec_bias, w_qkv, b_qkv, w_out, w_up, b_up, w_down):
    micro, local_len, local_seqs, width = acts_in.shape
    count_t = lax.axis_size("tensor")
    count_x = lax.axis_size("x")
    count_c = lax.axis_size("core")
    sections = lax.axis_size("section")
    section_index = lax.axis_index("section")
    length = local_len * count_t
    slots = -(-micro // count_t)
    padding = slots * count_t - micro
    head_dim = b_qkv.shape[2] * count_x * count_c // 3
    seqs = slots * local_seqs
    rows = seqs * length

    def features_in(value):
        lead = value.shape[:-1]
        value = value.reshape(*lead, count_x, count_c, -1)
        return jnp.swapaxes(value, -3, -2).reshape(*lead, width)

    def features_out(value):
        lead = value.shape[:-1]
        value = value.reshape(*lead, count_c, count_x, -1)
        return jnp.swapaxes(value, -3, -2).reshape(*lead, width)

    def collect(value):
        value = features_in(value)
        if padding:
            value = jnp.pad(value, ((0, padding), (0, 0), (0, 0), (0, 0)))
        value = value.reshape(count_t, slots, local_len, local_seqs, width)
        value = lax.all_to_all(value, "tensor", 0, 0, tiled=False)
        return value.transpose(1, 3, 0, 2, 4).reshape(rows, width)

    def give_back(value):
        value = value.reshape(slots, local_seqs, count_t, local_len, width)
        value = lax.all_to_all(value.transpose(2, 0, 3, 1, 4), "tensor", 0, 0, tiled=False)
        value = value.reshape(slots * count_t, local_len, local_seqs, width)[:micro]
        return features_out(value)

    packed = jnp.concatenate(
        [item[0].astype(F32).reshape(-1) for item in (norm_gains, vec_bias, b_qkv, b_up)]
    )
    every = lax.all_gather(packed, ("x", "core", "tensor"), axis=0, tiled=False)
    every = every.reshape(count_x, count_c, count_t, -1)
    sizes = [norm_gains.size, vec_bias.size, b_qkv.size, b_up.size]
    ends = [sum(sizes[: i + 1]) for i in range(len(sizes))]
    piece_gain, piece_shift, piece_bqkv, piece_bup = jnp.split(every, ends[:-1], axis=-1)

    def feature_vectors(piece, count):
        piece = piece.reshape(count_x, count_c, count_t, count, -1)
        return piece.transpose(3, 1, 0, 2, 4).reshape(count, width)

    def group_vectors(piece, shape):
        piece = piece.reshape(count_x, count_c, count_t, shape[1], shape[2])
        return piece.transpose(2, 3, 0, 1, 4).reshape(count_t, -1)

    gains = feature_vectors(piece_gain, norm_gains.shape[1])
    shifts = feature_vectors(piece_shift, vec_bias.shape[1])
    bias_qkv = group_vectors(piece_bqkv, b_qkv.shape)
    bias_up = group_vectors(piece_bup, b_up.shape)

    start_rows = collect(acts_in)

    def gather_rows(weight):
        stacked = gather_stack(gather_stack(gather_stack(weight, "tensor"), "x"), "core")
        shape = stacked.shape
        return jnp.moveaxis(stacked, 2, 0).reshape(count_t, -1, shape[-1])

    def gather_columns(weight):
        stacked = lax.all_gather(weight, "tensor", axis=0, tiled=True)
        stacked = gather_stack(gather_stack(stacked, "x"), "core")
        return stacked.reshape(count_c * count_x, -1, weight.shape[1])

    mat_qkv = gather_rows(w_qkv[0])
    mat_up = gather_rows(w_up[0])
    mat_out = gather_columns(w_out[0])
    mat_down = gather_columns(w_down[0])
    params = (gains, shifts, mat_qkv, bias_qkv, mat_out, mat_up, bias_up, mat_down)
    tables = rotation_tables(length, head_dim)

    inputs = start_rows
    for step in range(sections):
        result, stash = forward(inputs, params, tables, length, head_dim)
        if step < sections - 1:
            received = lax.ppermute(result, "section", [(i, i + 1) for i in range(sections - 1)])
            inputs = jnp.where(section_index == 0, start_rows, received)
    acts_local = give_back(result)

    end_rows = collect(cotangent)
    upstream = end_rows
    for step in range(sections):
        d_inputs, grads, small = backward(
            inputs, upstream, params, stash, tables, length, head_dim
        )
        if step < sections - 1:
            received = lax.ppermute(d_inputs, "section", [(i + 1, i) for i in range(sections - 1)])
            upstream = jnp.where(section_index == sections - 1, end_rows, received)
    grad_local = give_back(d_inputs)

    grad_qkv, grad_out, grad_up, grad_down = grads

    def share_rows(grad):
        grad = grad.reshape(count_t, count_c, count_x, -1, grad.shape[-1])
        grad = scatter_sum(jnp.moveaxis(grad, 1, 0), "core").astype(BF16)
        grad = scatter_sum(jnp.moveaxis(grad, 1, 0), "x")
        return lax.psum_scatter(
            grad.astype(BF16), "tensor", scatter_dimension=0, tiled=False
        ).astype(F32)

    def share_columns(grad):
        grad = grad.reshape(count_c, count_x, grad.shape[1], grad.shape[2])
        grad = scatter_sum(grad, "core").astype(BF16)
        grad = scatter_sum(grad, "x")
        return lax.psum_scatter(
            grad.astype(BF16), "tensor", scatter_dimension=0, tiled=True
        ).astype(F32)

    share_down = share_columns(grad_down)
    share_up = share_rows(grad_up)
    share_out = share_columns(grad_out)
    share_qkv = share_rows(grad_qkv)

    def feature_pieces(value):
        value = value.reshape(value.shape[0], count_c, count_x, count_t, -1)
        return value.transpose(2, 1, 3, 0, 4).reshape(count_x, count_c, count_t, -1)

    def group_pieces(value, shape):
        value = value.reshape(count_t, shape[1], count_x, count_c, shape[2])
        return value.transpose(2, 3, 0, 1, 4).reshape(count_x, count_c, count_t, -1)

    small_pieces = jnp.concatenate(
        [
            feature_pieces(small[0]),
            feature_pieces(small[1]),
            group_pieces(small[2], b_qkv.shape),
            group_pieces(small[3], b_up.shape),
        ],
        axis=-1,
    ).reshape(count_x * count_c * count_t, -1)
    share_small = lax.psum_scatter(
        small_pieces, ("x", "core", "tensor"), scatter_dimension=0, tiled=False
    )
    share_gain, share_shift, share_bqkv, share_bup = jnp.split(share_small, ends[:-1])
    return (
        acts_local[None],
        grad_local[None],
        share_gain.reshape(norm_gains.shape),
        share_shift.reshape(vec_bias.shape),
        share_qkv[None],
        share_bqkv.reshape(b_qkv.shape),
        share_out[None],
        share_up[None],
        share_bup.reshape(b_up.shape),
        share_down[None],
    )


def solution(mesh):
    sizes = mesh.shape
    cores = 2
    devices = mesh.devices.reshape(
        sizes["section"], sizes["dp"] // cores, cores, sizes["tensor"]
    )
    split = Mesh(devices, ("section", "x", "core", "tensor"))
    dp = ("x", "core")
    rows = P(None, "tensor", dp, None)
    vectors = P("section", None, ("x", "core", "tensor"))
    by_rows = P("section", dp, "tensor")
    by_columns = P("section", "tensor", dp)
    stacked = P("section", None, "tensor", dp, None)
    weights = (by_rows, by_columns, by_columns, by_rows, by_columns, by_columns)
    return jax.shard_map(
        local,
        mesh=split,
        in_specs=(rows, rows, vectors, vectors) + weights,
        out_specs=(stacked, stacked, vectors, vectors) + weights,
        check_vma=False,
    )
```
